128 devices in a mesh: heads: 4 (over x_hi, core), cells: 32 (over z, x_lo, y).
Axes of the slice: x: 4 (x_hi: 2, x_lo: 2; x = x_hi * 2 + x_lo), y: 4, z: 4, core: 2. Of those that a mesh axis runs over, the one named last changes fastest.
Arguments:
- cells_in: bfloat16 [8, 4096, 1024], P(None, ('heads', 'cells')), may hold values from -6 to 6
- gain: float32 [1024], replicated, may hold values from 0.1 to 1.9
- w_qkv: bfloat16 [1024, 3072], replicated
- w_out: bfloat16 [1024, 1024], replicated, may hold values from -0.1875 to 0.1875
- tile_of_cell: int32 [4096], P(('heads', 'cells')), may hold values from 0 to 255
- tile_adjacent: int32 [256, 256], replicated, may hold values from 0 to 1, as said below
Outputs:
- cells_out: bfloat16 [8, 4096, 1024], P(None, ('heads', 'cells'))
The draws below stay inside these ranges and needn't reach their ends.
Inputs may be any that keep to these rules, and one draw needn't show every extreme that they name: Tiles sit at the places of a 16 x 16 grid in an order drawn from the seed; tile_adjacent is 1 exactly where the two tiles' places differ by at most one in each grid direction, so it is symmetric with ones on the diagonal.
All inputs are finite; a program needn't handle non-finite values.
Results may differ from the reference program's by a relative error of at most 0.011.
Values may be sent and summed in bfloat16 or wider, within the bound.
A program may use at most 64 MiB of HBM per device.

```python
import math
import jax
import jax.numpy as jnp
from jax import lax

GENES = 8
HEADS = 16
HEAD_DIM = 64
D = 1024
CELLS = 4096
TSIDE = 16
TILES = 256


def draw_w_qkv(key, part):
    key_matrix = jax.random.split(jax.random.fold_in(key, 11), 3)
    w_query = jax.random.normal(key_matrix[0], (D, D), jnp.float32) * (2.0 / math.sqrt(D))
    w_key = jax.random.normal(key_matrix[1], (D, D), jnp.float32) * (1.0 / math.sqrt(D))
    w_value = jax.random.normal(key_matrix[2], (D, D), jnp.float32) * (1.0 / math.sqrt(D))
    return jnp.concatenate([w_query, w_key, w_value], axis=1).astype(jnp.bfloat16)


def draw_tile_adjacent(key, part):
    places = jax.random.permutation(jax.random.fold_in(key, 23), TILES)
    row_location = places // TSIDE
    col_pos = places % TSIDE
    near_rows = jnp.abs(row_location[:, None] - row_location[None, :]) <= 1
    neighbour_columns = jnp.abs(col_pos[:, None] - col_pos[None, :]) <= 1
    return (near_rows & neighbour_columns).astype(jnp.int32)


def touch_ends(result, key, low, largest):
    dims = result.shape
    place = [jax.random.randint(jax.random.fold_in(key, axis), (), 0, dims[axis]) for axis in range(len(dims))]
    result = result.at[tuple(place)].set(low)
    longest = dims.index(max(dims))
    place[longest] = (place[longest] + 1) % dims[longest]
    return result.at[tuple(place)].set(largest)


def block_scale(rng, extent, cuts, smallest, high):
    factor_of = 1.0
    for position, parts in cuts:
        draws = jax.random.uniform(jax.random.fold_in(jax.random.fold_in(rng, 6), position), (parts,), jnp.float32, smallest / len(cuts), high / len(cuts))
        factor_of = factor_of * jnp.repeat(jnp.exp(draws), extent[position] // parts).reshape((-1,) + (1,) * (len(extent) - 1 - position))
    return factor_of


def bell_draw(key, extent, scale, reach, shards=(), kind=jnp.bfloat16):
    entries = scale * jax.random.normal(key, extent, jnp.float32)
    if shards:
        entries = entries * block_scale(key, extent, shards, -0.22, 0.18)
    return jnp.clip(entries, -reach, reach).astype(kind)


def setup_inputs(seed: int = 0) -> dict:
    seeds = jax.random.split(jax.random.key(seed), 7)
    cells_in = bell_draw(seeds[0], (GENES, CELLS, D), 1.0, 6.0, ((1, 128),))
    gain = jnp.clip(1.0 + 0.18 * jax.random.normal(seeds[1], (D,), jnp.float32), 0.1, 1.9)
    w_qkv = draw_w_qkv(jax.random.fold_in(seeds[6], 71), 0)
    w_out = bell_draw(seeds[3], (D, D), D ** -0.5, 0.1875)
    tile_of_cell = touch_ends(jax.random.randint(seeds[4], (CELLS,), 0, TILES), jax.random.fold_in(seeds[4], 1), 0, TILES - 1).astype(jnp.int32)
    tile_adjacent = draw_tile_adjacent(jax.random.fold_in(seeds[6], 71), 0)
    return dict(cells_in=cells_in, gain=gain, w_qkv=w_qkv, w_out=w_out, tile_of_cell=tile_of_cell, tile_adjacent=tile_adjacent)


def attend_item(item, allowed):
    query_matrix, key_matrix, value_matrix = item
    logit_scores = jnp.dot(query_matrix, key_matrix.T, preferred_element_type=jnp.float32) * 0.125
    masked = jnp.where(allowed, logit_scores, -1e+30)
    top = lax.optimization_barrier(jnp.max(masked, axis=-1))
    softmax_weights = jnp.where(allowed, jnp.exp(masked - top[:, None]), 0.0)
    total = lax.optimization_barrier(jnp.sum(softmax_weights, axis=-1))
    summed = jnp.dot(softmax_weights.astype(jnp.bfloat16), value_matrix, preferred_element_type=jnp.float32)
    return (summed / total[:, None]).astype(jnp.bfloat16)

def reference(cells_in, gain, w_qkv, w_out, tile_of_cell, tile_adjacent):
    x32 = cells_in.astype(jnp.float32)
    normed = (x32 * lax.rsqrt(lax.optimization_barrier(jnp.mean(x32 * x32, axis=-1, keepdims=True)) + 1e-05) * gain).astype(jnp.bfloat16)
    qkv = jnp.dot(normed.reshape(GENES * CELLS, D), w_qkv, preferred_element_type=jnp.float32).astype(jnp.bfloat16)
    qkv = qkv.reshape(GENES, CELLS, 3, HEADS, HEAD_DIM).transpose(2, 0, 3, 1, 4).reshape(3, GENES * HEADS, CELLS, HEAD_DIM)
    allowed = tile_adjacent[tile_of_cell[:, None], tile_of_cell[None, :]].astype(jnp.int32)
    is_allowed = allowed > 0
    attended = lax.map(lambda item: attend_item(item, is_allowed), (qkv[0], qkv[1], qkv[2]))
    attended = attended.reshape(GENES, HEADS, CELLS, HEAD_DIM).transpose(0, 2, 1, 3).reshape(GENES * CELLS, D)
    attention_output = jnp.dot(attended, w_out, preferred_element_type=jnp.float32).astype(jnp.bfloat16)
    return attention_output.reshape(GENES, CELLS, D)
```

```python
import functools
import math

import jax
import jax.numpy as jnp
from jax import lax
from jax.experimental import pallas as pl
from jax.experimental.pallas import tpu as pltpu
from jax.sharding import PartitionSpec as P

MESH = pl.DeviceIdType.MESH
HD = 64
NDEV = 128
GENES = 8
HEADS = 16
ROWS = 32
HALF = 16
LANES = 128
GROUP = 16
NGROUP = NDEV // GROUP
TILE = 8
BIG = -1e30
QSCALE = 0.125 * math.log2(math.e)


def iota(shape, dim):
    return lax.broadcasted_iota(jnp.int32, shape, dim)


def dot(a, b):
    return jnp.dot(a, b, preferred_element_type=jnp.float32)


def dot_t(a, b):
    return lax.dot_general(a, b, (((1,), (1,)), ((), ())), preferred_element_type=jnp.float32)


def grid_places(adj):
    n = adj.shape[0]
    fi = lambda shape, dim: iota(shape, dim).astype(jnp.float32)
    degree = dot(jnp.ones((8, n), jnp.bfloat16), adj)
    corner = degree == 4.0
    before = (iota((n, n), 0) < iota((n, n), 1)).astype(jnp.bfloat16)
    order = dot(corner.astype(jnp.float32).astype(jnp.bfloat16), before)
    reach = jnp.where(corner & (order == fi((8, n), 0)), 1.0, 0.0)

    def step(_, state):
        reach, dist = state
        dist = dist + (1.0 - reach)
        return jnp.minimum(dot(reach.astype(jnp.bfloat16), adj), 1.0), dist

    reach, dist = lax.fori_loop(0, 14, step, (reach, jnp.zeros((8, n), jnp.float32)))
    dist = dist + (1.0 - reach)
    d0, d1, d2, d3 = (dist[i : i + 1] for i in range(4))
    on_path = lambda d: jnp.sum(jnp.where(d0 + d == 15.0, 1.0, 0.0), axis=1, keepdims=True)
    opp1, opp2 = on_path(d1) == 16.0, on_path(d2) == 16.0
    far = jnp.where(opp1, d1, jnp.where(opp2, d2, d3))
    side = jnp.where(opp1, d2, d1)
    other = jnp.where(opp1, d3, jnp.where(opp2, d3, d2))
    near = jnp.minimum(d0, side)
    row = jnp.where(near >= 8.0, near, 15.0 - jnp.minimum(other, far))
    near = jnp.minimum(d0, other)
    col = jnp.where(near >= 8.0, near, 15.0 - jnp.minimum(side, far))
    return row, col


def kernel(
    x_hbm, gain_ref, wqkv_hbm, wout_hbm, ids_ref, adj_ref, out_ref,
    x_buf, w_buf, wo_buf, norm_buf, send_buf, recv_buf, id_send, id_recv, table_buf,
    q_buf, k_buf, v_buf, m_buf, acc_buf, osend_buf, orecv_buf, att_buf,
    x_sem, w_sem, wo_sem, send_sem, recv_sem, idsend_sem, idrecv_sem, osend_sem, orecv_sem,
):
    hi = lax.axis_index("heads")
    ci = lax.axis_index("cells")
    me = hi * 32 + ci

    def device(p):
        return (p >> 5, p & 31)

    x_copy = pltpu.make_async_copy(x_hbm, x_buf, x_sem)
    x_copy.start()
    w_copies = []
    for c in range(4):
        for part in range(3):
            cp = pltpu.make_async_copy(
                wqkv_hbm.at[:, pl.ds(part * 1024 + c * 256, 256)], w_buf.at[c * 3 + part], w_sem.at[c * 3 + part]
            )
            cp.start()
            w_copies.append(cp)
    wo_copy = pltpu.make_async_copy(wout_hbm, wo_buf, wo_sem)
    wo_copy.start()

    barrier = pltpu.get_barrier_semaphore()

    def greet(k, _):
        pl.semaphore_signal(barrier, inc=1, device_id=device((me + k) & 127), device_id_type=MESH)
        return 0

    lax.fori_loop(1, NDEV, greet, 0)

    ids = ids_ref[...].astype(jnp.float32)
    ids = jnp.concatenate([ids, ids, ids, ids], axis=1)
    lane_row = iota((1, LANES), 1)
    for v in range(4):
        id_send[v] = jnp.where((lane_row >= 32 * v) & (lane_row < 32 * v + 32), ids, 0.0)

    x_copy.wait()
    x32 = x_buf[...].reshape(GENES * ROWS, 1024).astype(jnp.float32)
    mean = jnp.mean(x32 * x32, axis=-1, keepdims=True)
    norm_buf[...] = (x32 * lax.rsqrt(mean + 1e-05) * gain_ref[...]).astype(jnp.bfloat16)

    low = iota((GENES, ROWS, LANES), 2) < HD
    low_half = iota((GENES, HALF, LANES), 2) < HD
    xn = norm_buf[...]
    for c in range(4):
        for part in range(3):
            w_copies[c * 3 + part].wait()
        q4 = dot(xn, w_buf[c * 3]) * QSCALE
        k4 = dot(xn, w_buf[c * 3 + 1])
        v4 = dot(xn, w_buf[c * 3 + 2])
        for p in range(2):
            cut = lambda a: a[:, 128 * p : 128 * p + 128]
            swap = lambda a: pltpu.roll(a, HD, axis=1).reshape(GENES, ROWS, LANES)
            as3 = lambda a: a.reshape(GENES, ROWS, LANES)
            q2, k2, v2 = cut(q4), cut(k4), cut(v4)
            qs, ks, vs = swap(q2), swap(k2), swap(v2)
            q2, k2, v2 = as3(q2), as3(k2), as3(v2)
            head = 4 * c + 2 * p
            send_buf[:, head, 0:16, :] = jnp.where(low_half, q2[:, 0:16], qs[:, 16:32]).astype(jnp.bfloat16)
            send_buf[:, head, 16:48, :] = jnp.where(low, k2, vs).astype(jnp.bfloat16)
            send_buf[:, head + 1, 0:16, :] = jnp.where(low_half, qs[:, 0:16], q2[:, 16:32]).astype(jnp.bfloat16)
            send_buf[:, head + 1, 16:48, :] = jnp.where(low, ks, v2).astype(jnp.bfloat16)

    own = pltpu.make_async_copy(send_buf.at[me >> 4, me & 15], recv_buf.at[0], recv_sem.at[0])
    own.start()
    own_id = pltpu.make_async_copy(id_send.at[0], id_recv.at[0], idrecv_sem.at[0])
    own_id.start()
    pl.semaphore_wait(barrier, NDEV - 1)

    def send(k, _):
        p = (me + k) & 127
        pltpu.make_async_remote_copy(
            src_ref=id_send.at[k & 3], dst_ref=id_recv.at[k], send_sem=idsend_sem, recv_sem=idrecv_sem.at[k >> 4],
            device_id=device(p), device_id_type=MESH,
        ).start()
        pltpu.make_async_remote_copy(
            src_ref=send_buf.at[p >> 4, p & 15], dst_ref=recv_buf.at[k], send_sem=send_sem,
            recv_sem=recv_sem.at[k >> 4], device_id=device(p), device_id_type=MESH,
        ).start()
        return 0

    lax.fori_loop(1, NDEV, send, 0)

    row, col = grid_places(adj_ref[...].astype(jnp.float32).astype(jnp.bfloat16))
    place = iota((LANES, 256), 0).astype(jnp.float32)
    table_buf[...] = jnp.where((place == row + 64.0) | (place == col + 80.0), 1.0, 0.0).astype(jnp.bfloat16)
    ia, ib = iota((LANES, LANES), 0), iota((LANES, LANES), 1)
    same_part = (ia >= 64) & (ib >= 64) & (ia < 96) & (ib < 96) & ((ia < 80) == (ib < 80))
    penalty = jnp.where(same_part & (jnp.abs(ia - ib) > 1), BIG, 0.0).astype(jnp.bfloat16)

    m_buf[...] = jnp.full(m_buf.shape, BIG, jnp.float32)
    acc_buf[...] = jnp.zeros(acc_buf.shape, jnp.float32)

    def prepare(g):
        pltpu.make_async_copy(id_recv.at[pl.ds(0, GROUP)], id_recv.at[pl.ds(0, GROUP)], idrecv_sem.at[g]).wait()
        pltpu.make_async_copy(recv_buf.at[pl.ds(0, GROUP)], recv_buf.at[pl.ds(0, GROUP)], recv_sem.at[g]).wait()
        tile_no = iota((256, LANES), 0).astype(jnp.float32)
        low4 = iota((4, ROWS, LANES), 2) < HD
        low4h = iota((4, HALF, LANES), 2) < HD
        for part in range(4):
            s = g * GROUP + 4 * part
            cell_ids = id_recv[s] + id_recv[s + 1] + id_recv[s + 2] + id_recv[s + 3]
            hot = jnp.where(tile_no == cell_ids, 1.0, 0.0).astype(jnp.bfloat16)
            codes = dot(table_buf[...], hot).T
            fines = dot(codes.astype(jnp.bfloat16), penalty).reshape(4, ROWS, LANES)
            codes = codes.reshape(4, ROWS, LANES)
            block = recv_buf[pl.ds(s, 4)].astype(jnp.float32)
            kv = block[:, 16:48]
            qq = block[:, 0:16]
            qr = pltpu.roll(qq.reshape(4 * HALF, LANES), HD, axis=1).reshape(4, HALF, LANES)
            k_buf[pl.ds(s, 4)] = jnp.where(low4, kv, codes).astype(jnp.bfloat16)
            v_buf[pl.ds(s, 4)] = jnp.where(low4, 1.0, kv).astype(jnp.bfloat16)
            q_buf[pl.ds(s, 4), 0:16] = jnp.where(low4h, qq, fines[:, 0:16]).astype(jnp.bfloat16)
            q_buf[pl.ds(s, 4), 16:32] = jnp.where(low4h, qr, fines[:, 16:32]).astype(jnp.bfloat16)

    qn, kn = TILE * ROWS, GROUP * ROWS

    def update(t, j):
        q = q_buf[pl.ds(t * TILE, TILE)].reshape(qn, LANES)
        k = k_buf[pl.ds(j * GROUP, GROUP)].reshape(kn, LANES)
        v = v_buf[pl.ds(j * GROUP, GROUP)].reshape(kn, LANES)
        s = dot_t(q, k)
        rows = pl.ds(pl.multiple_of(t * qn, qn), qn)
        m_old = m_buf[rows]
        m_new = jnp.maximum(m_old, jnp.max(s, axis=1, keepdims=True))
        m_buf[rows] = m_new
        w = jnp.exp2(s - jnp.concatenate([m_new] * (kn // LANES), axis=1)).astype(jnp.bfloat16)
        acc_buf[rows] = acc_buf[rows] * jnp.exp2(m_old - m_new) + dot(w, v)

    def finish(t):
        rows = pl.ds(pl.multiple_of(t * qn, qn), qn)
        acc = acc_buf[rows]
        swapped = pltpu.roll(acc, HD, axis=1)
        lo = iota((qn, LANES), 1) < HD
        res = jnp.where(lo, swapped, acc) / jnp.where(lo, acc, swapped)
        res = res.reshape(TILE, ROWS, LANES)
        lo = iota((TILE, HALF, LANES), 2) < HD
        osend_buf[pl.ds(t * TILE, TILE)] = jnp.where(lo, res[:, 0:16], res[:, 16:32]).astype(jnp.bfloat16)

        def give(i, _):
            k = t * TILE + i
            p = (me - k) & 127

            @pl.when(k > 0)
            def _():
                pltpu.make_async_remote_copy(
                    src_ref=osend_buf.at[k], dst_ref=orecv_buf.at[me >> 4, me & 15], send_sem=osend_sem,
                    recv_sem=orecv_sem, device_id=device(p), device_id_type=MESH,
                ).start()

            @pl.when(k == 0)
            def _():
                pltpu.make_async_copy(osend_buf.at[0], orecv_buf.at[me >> 4, me & 15], orecv_sem).start()

            return 0

        lax.fori_loop(0, TILE, give, 0)

    def group_step(g, _):
        prepare(g)

        def old(t, _):
            update(t, g)
            return 0

        lax.fori_loop(0, 2 * g, old, 0)

        def new(i, _):
            update(2 * g + (i & 1), i >> 1)
            return 0

        lax.fori_loop(0, 2 * g + 2, new, 0)
        return 0

    last = NGROUP - 1
    lax.fori_loop(0, last, group_step, 0)
    prepare(last)

    def old_last(t, _):
        update(t, last)
        finish(t)
        return 0

    lax.fori_loop(0, 2 * last, old_last, 0)

    def new_last(t, _):
        def inner(j, _):
            update(t, j)
            return 0

        lax.fori_loop(0, NGROUP, inner, 0)
        finish(t)
        return 0

    lax.fori_loop(2 * last, 2 * NGROUP, new_last, 0)

    wo_copy.wait()
    pltpu.make_async_copy(orecv_buf, orecv_buf, orecv_sem).wait()
    lo = iota((GENES, HALF, LANES), 2) < HD
    for p in range(HEADS // 2):
        even = orecv_buf[:, 2 * p].astype(jnp.float32)
        odd = orecv_buf[:, 2 * p + 1].astype(jnp.float32)
        swap = lambda a: pltpu.roll(a.reshape(GENES * HALF, LANES), HD, axis=1).reshape(GENES, HALF, LANES)
        att_buf[:, 0:16, 128 * p : 128 * p + 128] = jnp.where(lo, even, swap(odd)).astype(jnp.bfloat16)
        att_buf[:, 16:32, 128 * p : 128 * p + 128] = jnp.where(lo, swap(even), odd).astype(jnp.bfloat16)
    att = att_buf[...].reshape(GENES * ROWS, 1024)
    for c in range(4):
        part = dot(att, wo_buf[:, 256 * c : 256 * c + 256])
        out_ref[:, :, 256 * c : 256 * c + 256] = part.astype(jnp.bfloat16).reshape(GENES, ROWS, 256)

    pltpu.make_async_copy(recv_buf.at[pl.ds(0, 127)], recv_buf.at[pl.ds(0, 127)], send_sem).wait()
    pltpu.make_async_copy(id_recv.at[pl.ds(0, 127)], id_recv.at[pl.ds(0, 127)], idsend_sem).wait()
    pltpu.make_async_copy(osend_buf.at[pl.ds(0, 127)], osend_buf.at[pl.ds(0, 127)], osend_sem).wait()


def on_device(cells_in, gain, w_qkv, w_out, tile_of_cell, tile_adjacent):
    bf, f32 = jnp.bfloat16, jnp.float32
    vm = pltpu.VMEM
    hbm = pl.BlockSpec(memory_space=pl.ANY)
    vmem = pl.BlockSpec(memory_space=pltpu.VMEM)
    return pl.pallas_call(
        kernel,
        out_shape=jax.ShapeDtypeStruct(cells_in.shape, bf),
        in_specs=[hbm, vmem, hbm, hbm, vmem, vmem],
        out_specs=vmem,
        scratch_shapes=[
            vm((GENES, ROWS, 1024), bf),
            vm((12, 1024, 256), bf),
            vm((1024, 1024), bf),
            vm((GENES * ROWS, 1024), bf),
            vm((GENES, HEADS, 48, LANES), bf),
            vm((NDEV, 48, LANES), bf),
            vm((4, 1, LANES), f32),
            vm((NDEV, 1, LANES), f32),
            vm((LANES, 256), bf),
            vm((NDEV, ROWS, LANES), bf),
            vm((NDEV, ROWS, LANES), bf),
            vm((NDEV, ROWS, LANES), bf),
            vm((NDEV * ROWS, LANES), f32),
            vm((NDEV * ROWS, LANES), f32),
            vm((NDEV, HALF, LANES), bf),
            vm((GENES, HEADS, HALF, LANES), bf),
            vm((GENES, ROWS, 1024), bf),
            pltpu.SemaphoreType.DMA,
            pltpu.SemaphoreType.DMA((12,)),
            pltpu.SemaphoreType.DMA,
            pltpu.SemaphoreType.DMA,
            pltpu.SemaphoreType.DMA((NGROUP,)),
            pltpu.SemaphoreType.DMA,
            pltpu.SemaphoreType.DMA((NGROUP,)),
            pltpu.SemaphoreType.DMA,
            pltpu.SemaphoreType.DMA,
        ],
        compiler_params=pltpu.CompilerParams(
            collective_id=0, has_side_effects=True, vmem_limit_bytes=56 * 1024 * 1024
        ),
    )(cells_in, gain.reshape(1, -1), w_qkv, w_out, tile_of_cell.reshape(1, -1), tile_adjacent)


def solution(mesh):
    return jax.shard_map(
        on_device,
        mesh=mesh,
        in_specs=(P(None, ("heads", "cells"), None), P(), P(), P(), P(("heads", "cells")), P()),
        out_specs=P(None, ("heads", "cells"), None),
        check_vma=False,
    )
```

```python
import functools
import math

import jax
import jax.numpy as jnp
from jax import lax
from jax.experimental import pallas as pl
from jax.experimental.pallas import tpu as pltpu
from jax.sharding import PartitionSpec as P

MESH = pl.DeviceIdType.MESH
HD = 64
NDEV = 128
GENES = 8
HEADS = 16
ROWS = 32
HALF = 16
LANES = 128
GROUP = 16
NGROUP = NDEV // GROUP
CELLS = GROUP * ROWS
BIG = -1e30
QSCALE = 0.125 * math.log2(math.e)


def iota(shape, dim):
    return lax.broadcasted_iota(jnp.int32, shape, dim)


def dot(a, b):
    return jnp.dot(a, b, preferred_element_type=jnp.float32)


def dot_t(a, b):
    return lax.dot_general(a, b, (((1,), (1,)), ((), ())), preferred_element_type=jnp.float32)


def grid_places(adj):
    n = adj.shape[0]
    fi = lambda shape, dim: iota(shape, dim).astype(jnp.float32)
    degree = dot(jnp.ones((8, n), jnp.bfloat16), adj)
    corner = degree == 4.0
    before = (iota((n, n), 0) < iota((n, n), 1)).astype(jnp.bfloat16)
    order = dot(corner.astype(jnp.float32).astype(jnp.bfloat16), before)
    reach = jnp.where(corner & (order == fi((8, n), 0)), 1.0, 0.0)

    def step(_, state):
        reach, dist = state
        dist = dist + (1.0 - reach)
        return jnp.minimum(dot(reach.astype(jnp.bfloat16), adj), 1.0), dist

    reach, dist = lax.fori_loop(0, 14, step, (reach, jnp.zeros((8, n), jnp.float32)))
    dist = dist + (1.0 - reach)
    d0, d1, d2, d3 = (dist[i : i + 1] for i in range(4))
    on_path = lambda d: jnp.sum(jnp.where(d0 + d == 15.0, 1.0, 0.0), axis=1, keepdims=True)
    opp1, opp2 = on_path(d1) == 16.0, on_path(d2) == 16.0
    far = jnp.where(opp1, d1, jnp.where(opp2, d2, d3))
    side = jnp.where(opp1, d2, d1)
    other = jnp.where(opp1, d3, jnp.where(opp2, d3, d2))
    near = jnp.minimum(d0, side)
    row = jnp.where(near >= 8.0, near, 15.0 - jnp.minimum(other, far))
    near = jnp.minimum(d0, other)
    col = jnp.where(near >= 8.0, near, 15.0 - jnp.minimum(side, far))
    return row, col


def kernel(
    x_hbm, gain_ref, wqkv_hbm, wout_hbm, ids_ref, adj_ref, out_ref,
    x_buf, w_buf, wo_buf, norm_buf, send_buf, recv_buf, id_send, id_recv, table_buf,
    q_buf, k_buf, v_buf, s_buf, m_buf, acc_buf, osend_buf, orecv_buf, att_buf,
    x_sem, w_sem, wo_sem, send_sem, recv_sem, idsend_sem, idrecv_sem, osend_sem, orecv_sem,
):
    hi = lax.axis_index("heads")
    ci = lax.axis_index("cells")
    me = hi * 32 + ci

    def device(p):
        return (p >> 5, p & 31)

    x_copy = pltpu.make_async_copy(x_hbm, x_buf, x_sem)
    x_copy.start()
    w_copies = []
    for c in range(4):
        for part in range(3):
            cp = pltpu.make_async_copy(
                wqkv_hbm.at[:, pl.ds(part * 1024 + c * 256, 256)], w_buf.at[c * 3 + part], w_sem.at[c * 3 + part]
            )
            cp.start()
            w_copies.append(cp)
    wo_copy = pltpu.make_async_copy(wout_hbm, wo_buf, wo_sem)
    wo_copy.start()

    barrier = pltpu.get_barrier_semaphore()

    def greet(k, _):
        pl.semaphore_signal(barrier, inc=1, device_id=device((me + k) & 127), device_id_type=MESH)
        return 0

    lax.fori_loop(1, NDEV, greet, 0)

    ids = ids_ref[...].astype(jnp.float32)
    ids = jnp.concatenate([ids, ids, ids, ids], axis=1)
    lane_row = iota((1, LANES), 1)
    for v in range(4):
        id_send[v] = jnp.where((lane_row >= 32 * v) & (lane_row < 32 * v + 32), ids, 0.0)

    x_copy.wait()
    x32 = x_buf[...].reshape(GENES * ROWS, 1024).astype(jnp.float32)
    mean = jnp.mean(x32 * x32, axis=-1, keepdims=True)
    norm_buf[...] = (x32 * lax.rsqrt(mean + 1e-05) * gain_ref[...]).astype(jnp.bfloat16)

    low = iota((GENES, ROWS, LANES), 2) < HD
    low_half = iota((GENES, HALF, LANES), 2) < HD
    xn = norm_buf[...]
    for c in range(4):
        for part in range(3):
            w_copies[c * 3 + part].wait()
        q4 = dot(xn, w_buf[c * 3]) * QSCALE
        k4 = dot(xn, w_buf[c * 3 + 1])
        v4 = dot(xn, w_buf[c * 3 + 2])
        for p in range(2):
            cut = lambda a: a[:, 128 * p : 128 * p + 128]
            swap = lambda a: pltpu.roll(a, HD, axis=1).reshape(GENES, ROWS, LANES)
            as3 = lambda a: a.reshape(GENES, ROWS, LANES)
            q2, k2, v2 = cut(q4), cut(k4), cut(v4)
            qs, ks, vs = swap(q2), swap(k2), swap(v2)
            q2, k2, v2 = as3(q2), as3(k2), as3(v2)
            head = 4 * c + 2 * p
            send_buf[:, head, 0:16, :] = jnp.where(low_half, q2[:, 0:16], qs[:, 16:32]).astype(jnp.bfloat16)
            send_buf[:, head, 16:48, :] = jnp.where(low, k2, vs).astype(jnp.bfloat16)
            send_buf[:, head + 1, 0:16, :] = jnp.where(low_half, qs[:, 0:16], q2[:, 16:32]).astype(jnp.bfloat16)
            send_buf[:, head + 1, 16:48, :] = jnp.where(low, ks, v2).astype(jnp.bfloat16)

    own = pltpu.make_async_copy(send_buf.at[me >> 4, me & 15], recv_buf.at[0], recv_sem.at[0])
    own.start()
    own_id = pltpu.make_async_copy(id_send.at[0], id_recv.at[0], idrecv_sem.at[0])
    own_id.start()
    pl.semaphore_wait(barrier, NDEV - 1)

    def send(k, _):
        p = (me + k) & 127
        pltpu.make_async_remote_copy(
            src_ref=id_send.at[k & 3], dst_ref=id_recv.at[k], send_sem=idsend_sem, recv_sem=idrecv_sem.at[k >> 4],
            device_id=device(p), device_id_type=MESH,
        ).start()
        pltpu.make_async_remote_copy(
            src_ref=send_buf.at[p >> 4, p & 15], dst_ref=recv_buf.at[k], send_sem=send_sem,
            recv_sem=recv_sem.at[k >> 4], device_id=device(p), device_id_type=MESH,
        ).start()
        return 0

    lax.fori_loop(1, NDEV, send, 0)

    row, col = grid_places(adj_ref[...].astype(jnp.float32).astype(jnp.bfloat16))
    place = iota((LANES, 256), 0).astype(jnp.float32)
    table_buf[...] = jnp.where((place == row + 64.0) | (place == col + 80.0), 1.0, 0.0).astype(jnp.bfloat16)
    ia, ib = iota((LANES, LANES), 0), iota((LANES, LANES), 1)
    same_part = (ia >= 64) & (ib >= 64) & (ia < 96) & (ib < 96) & ((ia < 80) == (ib < 80))
    penalty = jnp.where(same_part & (jnp.abs(ia - ib) > 1), BIG, 0.0).astype(jnp.bfloat16)

    m_buf[...] = jnp.full(m_buf.shape, BIG, jnp.float32)
    acc_buf[...] = jnp.zeros(acc_buf.shape, jnp.float32)

    def prepare(g):
        pltpu.make_async_copy(id_recv.at[pl.ds(0, GROUP)], id_recv.at[pl.ds(0, GROUP)], idrecv_sem.at[g]).wait()
        pltpu.make_async_copy(recv_buf.at[pl.ds(0, GROUP)], recv_buf.at[pl.ds(0, GROUP)], recv_sem.at[g]).wait()
        tile_no = iota((256, LANES), 0).astype(jnp.float32)
        low4 = iota((4, ROWS, LANES), 2) < HD
        low4h = iota((4, HALF, LANES), 2) < HD
        for part in range(4):
            s = g * GROUP + 4 * part
            cell_ids = id_recv[s] + id_recv[s + 1] + id_recv[s + 2] + id_recv[s + 3]
            hot = jnp.where(tile_no == cell_ids, 1.0, 0.0).astype(jnp.bfloat16)
            codes = dot(table_buf[...], hot).T
            fines = dot(codes.astype(jnp.bfloat16), penalty).reshape(4, ROWS, LANES)
            codes = codes.reshape(4, ROWS, LANES)
            block = recv_buf[pl.ds(s, 4)].astype(jnp.float32)
            kv = block[:, 16:48]
            qq = block[:, 0:16]
            qr = pltpu.roll(qq.reshape(4 * HALF, LANES), HD, axis=1).reshape(4, HALF, LANES)
            k_buf[pl.ds(s, 4)] = jnp.where(low4, kv, codes).astype(jnp.bfloat16)
            v_buf[g, 0:64, 128 * part : 128 * part + 128] = kv.reshape(4 * ROWS, LANES).T[64:128].astype(jnp.bfloat16)
            q_buf[pl.ds(s, 4), 0:16] = jnp.where(low4h, qq, fines[:, 0:16]).astype(jnp.bfloat16)
            q_buf[pl.ds(s, 4), 16:32] = jnp.where(low4h, qr, fines[:, 16:32]).astype(jnp.bfloat16)
        v_buf[g, 64:80, :] = jnp.ones((16, CELLS), jnp.bfloat16)

    def score(item, slot):
        t, j = item
        q = q_buf[pl.ds(t * GROUP, GROUP)].reshape(CELLS, LANES)
        k = k_buf[pl.ds(j * GROUP, GROUP)].reshape(CELLS, LANES)
        s_buf[slot] = dot_t(k, q)

    def update(item, slot, following=None):
        t, j = item
        if following is not None:
            score(following, 1 - slot)
        s = s_buf[slot]
        m_old = m_buf[t]
        m_new = jnp.maximum(m_old, jnp.max(s, axis=0, keepdims=True))
        w = jnp.exp2(s - m_new[0:1]).astype(jnp.bfloat16)
        acc = acc_buf[t] * jnp.exp2(m_old - m_new)[0:1] + dot(v_buf[j], w)
        m_buf[t] = m_new
        acc_buf[t] = acc

    def finish(t):
        acc = acc_buf[t]
        res = acc[0:64] / acc[64:65]
        res = jnp.concatenate([res, res], axis=0).T.reshape(GROUP, ROWS, LANES)
        lo = iota((GROUP, HALF, LANES), 2) < HD
        osend_buf[pl.ds(t * GROUP, GROUP)] = jnp.where(lo, res[:, 0:16], res[:, 16:32]).astype(jnp.bfloat16)

        def give(i, _):
            k = t * GROUP + i
            p = (me - k) & 127

            @pl.when(k > 0)
            def _():
                pltpu.make_async_remote_copy(
                    src_ref=osend_buf.at[k], dst_ref=orecv_buf.at[me >> 4, me & 15], send_sem=osend_sem,
                    recv_sem=orecv_sem, device_id=device(p), device_id_type=MESH,
                ).start()

            @pl.when(k == 0)
            def _():
                pltpu.make_async_copy(osend_buf.at[0], orecv_buf.at[me >> 4, me & 15], orecv_sem).start()

            return 0

        lax.fori_loop(0, GROUP, give, 0)

    def group_step(g, _):
        prepare(g)

        def item(i):
            return (jnp.where(i < g, i, g), jnp.where(i < g, g, i - g))

        score(item(0), 0)

        def two(i, _):
            update(item(2 * i), 0, item(2 * i + 1))
            update(item(2 * i + 1), 1, item(2 * i + 2))
            return 0

        lax.fori_loop(0, g, two, 0)
        update((g, g), 0)
        return 0

    last = NGROUP - 1
    lax.fori_loop(0, last, group_step, 0)
    prepare(last)
    score((0, last), 0)

    def two_old(i, _):
        update((2 * i, last), 0, (2 * i + 1, last))
        finish(2 * i)
        update((2 * i + 1, last), 1, (2 * i + 2, last))
        finish(2 * i + 1)
        return 0

    lax.fori_loop(0, last // 2, two_old, 0)
    update((last - 1, last), 0, (last, 0))
    finish(last - 1)

    def two_new(i, _):
        update((last, 2 * i), 1, (last, 2 * i + 1))
        update((last, 2 * i + 1), 0, (last, jnp.minimum(2 * i + 2, last)))
        return 0

    lax.fori_loop(0, NGROUP // 2, two_new, 0)
    finish(last)

    wo_copy.wait()
    pltpu.make_async_copy(orecv_buf, orecv_buf, orecv_sem).wait()
    lo = iota((GENES, HALF, LANES), 2) < HD
    for p in range(HEADS // 2):
        even = orecv_buf[:, 2 * p].astype(jnp.float32)
        odd = orecv_buf[:, 2 * p + 1].astype(jnp.float32)
        swap = lambda a: pltpu.roll(a.reshape(GENES * HALF, LANES), HD, axis=1).reshape(GENES, HALF, LANES)
        att_buf[:, 0:16, 128 * p : 128 * p + 128] = jnp.where(lo, even, swap(odd)).astype(jnp.bfloat16)
        att_buf[:, 16:32, 128 * p : 128 * p + 128] = jnp.where(lo, swap(even), odd).astype(jnp.bfloat16)
    att = att_buf[...].reshape(GENES * ROWS, 1024)
    for c in range(4):
        part = dot(att, wo_buf[:, 256 * c : 256 * c + 256])
        out_ref[:, :, 256 * c : 256 * c + 256] = part.astype(jnp.bfloat16).reshape(GENES, ROWS, 256)

    pltpu.make_async_copy(recv_buf.at[pl.ds(0, 127)], recv_buf.at[pl.ds(0, 127)], send_sem).wait()
    pltpu.make_async_copy(id_recv.at[pl.ds(0, 127)], id_recv.at[pl.ds(0, 127)], idsend_sem).wait()
    pltpu.make_async_copy(osend_buf.at[pl.ds(0, 127)], osend_buf.at[pl.ds(0, 127)], osend_sem).wait()


def on_device(cells_in, gain, w_qkv, w_out, tile_of_cell, tile_adjacent):
    bf, f32 = jnp.bfloat16, jnp.float32
    vm = pltpu.VMEM
    hbm = pl.BlockSpec(memory_space=pl.ANY)
    vmem = pl.BlockSpec(memory_space=pltpu.VMEM)
    return pl.pallas_call(
        kernel,
        out_shape=jax.ShapeDtypeStruct(cells_in.shape, bf),
        in_specs=[hbm, vmem, hbm, hbm, vmem, vmem],
        out_specs=vmem,
        scratch_shapes=[
            vm((GENES, ROWS, 1024), bf),
            vm((12, 1024, 256), bf),
            vm((1024, 1024), bf),
            vm((GENES * ROWS, 1024), bf),
            vm((GENES, HEADS, 48, LANES), bf),
            vm((NDEV, 48, LANES), bf),
            vm((4, 1, LANES), f32),
            vm((NDEV, 1, LANES), f32),
            vm((LANES, 256), bf),
            vm((NDEV, ROWS, LANES), bf),
            vm((NDEV, ROWS, LANES), bf),
            vm((NGROUP, 80, CELLS), bf),
            vm((2, CELLS, CELLS), f32),
            vm((NGROUP, 8, CELLS), f32),
            vm((NGROUP, 80, CELLS), f32),
            vm((NDEV, HALF, LANES), bf),
            vm((GENES, HEADS, HALF, LANES), bf),
            vm((GENES, ROWS, 1024), bf),
            pltpu.SemaphoreType.DMA,
            pltpu.SemaphoreType.DMA((12,)),
            pltpu.SemaphoreType.DMA,
            pltpu.SemaphoreType.DMA,
            pltpu.SemaphoreType.DMA((NGROUP,)),
            pltpu.SemaphoreType.DMA,
            pltpu.SemaphoreType.DMA((NGROUP,)),
            pltpu.SemaphoreType.DMA,
            pltpu.SemaphoreType.DMA,
        ],
        compiler_params=pltpu.CompilerParams(
            collective_id=0, has_side_effects=True, vmem_limit_bytes=56 * 1024 * 1024
        ),
    )(cells_in, gain.reshape(1, -1), w_qkv, w_out, tile_of_cell.reshape(1, -1), tile_adjacent)


def solution(mesh):
    return jax.shard_map(
        on_device,
        mesh=mesh,
        in_specs=(P(None, ("heads", "cells"), None), P(), P(), P(), P(("heads", "cells")), P()),
        out_specs=P(None, ("heads", "cells"), None),
        check_vma=False,
    )
```

```python
import functools
import math

import jax
import jax.numpy as jnp
from jax import lax
from jax.experimental import pallas as pl
from jax.experimental.pallas import tpu as pltpu
from jax.sharding import PartitionSpec as P

MESH = pl.DeviceIdType.MESH
HD = 64
NDEV = 128
GENES = 8
HEADS = 16
ROWS = 32
HALF = 16
LANES = 128
GROUP = 32
NGROUP = NDEV // GROUP
FIRST, SECOND, THIRD = 16, 32, 64
STEPS = 2
PER_STEP = (NDEV - THIRD) // STEPS
CELLS = GROUP * ROWS
QT = 16
QC = QT * ROWS
NT = NDEV // QT
BIG = -1e30
QSCALE = 0.125 * math.log2(math.e)


def iota(shape, dim):
    return lax.broadcasted_iota(jnp.int32, shape, dim)


def dot(a, b):
    return jnp.dot(a, b, preferred_element_type=jnp.float32)


def dot_t(a, b):
    return lax.dot_general(a, b, (((1,), (1,)), ((), ())), preferred_element_type=jnp.float32)


def grid_places(adj):
    n = adj.shape[0]
    fi = lambda shape, dim: iota(shape, dim).astype(jnp.float32)
    degree = dot(jnp.ones((8, n), jnp.bfloat16), adj)
    corner = degree == 4.0
    before = (iota((n, n), 0) < iota((n, n), 1)).astype(jnp.bfloat16)
    order = dot(corner.astype(jnp.float32).astype(jnp.bfloat16), before)
    reach = jnp.where(corner & (order == fi((8, n), 0)), 1.0, 0.0)

    def step(_, state):
        reach, dist = state
        dist = dist + (1.0 - reach)
        return jnp.minimum(dot(reach.astype(jnp.bfloat16), adj), 1.0), dist

    dist = jnp.zeros((8, n), jnp.float32)
    for i in range(14):
        reach, dist = step(i, (reach, dist))
    dist = dist + (1.0 - reach)
    d0, d1, d2, d3 = (dist[i : i + 1] for i in range(4))
    on_path = lambda d: jnp.sum(jnp.where(d0 + d == 15.0, 1.0, 0.0), axis=1, keepdims=True)
    opp1, opp2 = on_path(d1) == 16.0, on_path(d2) == 16.0
    far = jnp.where(opp1, d1, jnp.where(opp2, d2, d3))
    side = jnp.where(opp1, d2, d1)
    other = jnp.where(opp1, d3, jnp.where(opp2, d3, d2))
    near = jnp.minimum(d0, side)
    row = jnp.where(near >= 8.0, near, 15.0 - jnp.minimum(other, far))
    near = jnp.minimum(d0, other)
    col = jnp.where(near >= 8.0, near, 15.0 - jnp.minimum(side, far))
    return row, col


def kernel(
    x_hbm, gain_ref, wqkv_hbm, ids_ref, adj_ref, att_buf,
    x_buf, w_buf, norm_buf, send_buf, recv_buf, id_near, id_send, id_recv, table_buf,
    q_buf, k_buf, v_buf, s_buf, m_buf, acc_buf, osend_buf, orecv_buf,
    x_sem, w_sem, send_sem, recv_sem, idsend_sem, idrecv_sem, osend_sem, orecv_sem,
):
    hi = lax.axis_index("heads")
    ci = lax.axis_index("cells")
    me = hi * 32 + ci

    def device(p):
        return (p >> 5, p & 31)

    z, y, x, core = ci >> 3, ci & 3, (hi & 2) | ((ci >> 2) & 1), hi & 1

    def moved(k, sign):
        dx, dy, dz = (k >> 2) & 3, k & 3, (k >> 5) + ((k >> 2) & 3) + (k & 3)
        px, py, pz = (x + sign * dx) & 3, (y + sign * dy) & 3, (z + sign * dz) & 3
        return ((px & 2) | (core ^ ((k >> 4) & 1)), pz * 8 + (px & 1) * 4 + py)

    def target(k):
        return moved(k, 1)

    def source(k):
        return moved(k, -1)

    x_copy = pltpu.make_async_copy(x_hbm, x_buf, x_sem)
    x_copy.start()
    w_copies = []
    for c in range(4):
        for part in range(3):
            cp = pltpu.make_async_copy(
                wqkv_hbm.at[:, pl.ds(part * 1024 + c * 256, 256)], w_buf.at[c * 3 + part], w_sem.at[c * 3 + part]
            )
            cp.start()
            w_copies.append(cp)

    barrier = pltpu.get_barrier_semaphore()

    def greet(k, _):
        pl.semaphore_signal(barrier, inc=1, device_id=device((me + k) & 127), device_id_type=MESH)
        return 0

    lax.fori_loop(1, NDEV, greet, 0)

    ids = ids_ref[...].astype(jnp.float32)
    id_near[hi] = jnp.concatenate([ids, jnp.zeros((1, 96), jnp.float32)], axis=1)

    x_copy.wait()
    x32 = x_buf[...].reshape(GENES * ROWS, 1024).astype(jnp.float32)
    mean = jnp.mean(x32 * x32, axis=-1, keepdims=True)
    norm_buf[...] = (x32 * lax.rsqrt(mean + 1e-05) * gain_ref[...]).astype(jnp.bfloat16)

    low = iota((GENES, ROWS, LANES), 2) < HD
    low_half = iota((GENES, HALF, LANES), 2) < HD
    xn = norm_buf[...]
    for cp in w_copies:
        cp.wait()
    row, col = grid_places(adj_ref[...].astype(jnp.float32).astype(jnp.bfloat16))
    place = iota((LANES, 256), 0).astype(jnp.float32)
    table_buf[...] = jnp.where((place == row + 64.0) | (place == col + 80.0), 1.0, 0.0).astype(jnp.bfloat16)
    for c in range(4):
        q4 = dot(xn, w_buf[c * 3]) * QSCALE
        k4 = dot(xn, w_buf[c * 3 + 1])
        v4 = dot(xn, w_buf[c * 3 + 2])
        for p in range(2):
            cut = lambda a: a[:, 128 * p : 128 * p + 128]
            swap = lambda a: pltpu.roll(a, HD, axis=1).reshape(GENES, ROWS, LANES)
            as3 = lambda a: a.reshape(GENES, ROWS, LANES)
            q2, k2, v2 = cut(q4), cut(k4), cut(v4)
            qs, ks, vs = swap(q2), swap(k2), swap(v2)
            q2, k2, v2 = as3(q2), as3(k2), as3(v2)
            head = 4 * c + 2 * p
            send_buf[:, head, 0:16, :] = jnp.where(low_half, q2[:, 0:16], qs[:, 16:32]).astype(jnp.bfloat16)
            send_buf[:, head, 16:48, :] = jnp.where(low, k2, vs).astype(jnp.bfloat16)
            send_buf[:, head + 1, 0:16, :] = jnp.where(low_half, qs[:, 0:16], q2[:, 16:32]).astype(jnp.bfloat16)
            send_buf[:, head + 1, 16:48, :] = jnp.where(low, ks, v2).astype(jnp.bfloat16)

    own = pltpu.make_async_copy(send_buf.at[me >> 4, me & 15], recv_buf.at[0], recv_sem.at[0])
    own.start()
    pl.semaphore_wait(barrier, NDEV - 1)

    def id_copy_near(k):
        return pltpu.make_async_remote_copy(
            src_ref=id_near.at[hi], dst_ref=id_near.at[hi], send_sem=idsend_sem.at[0], recv_sem=idrecv_sem.at[0],
            device_id=((hi + k) & 3, ci), device_id_type=MESH,
        )

    for k in range(1, 4):
        id_copy_near(k).start()

    def send(k, _):
        th, tc = target(k)
        pltpu.make_async_remote_copy(
            src_ref=send_buf.at[th * 2 + (tc >> 4), tc & 15], dst_ref=recv_buf.at[k], send_sem=send_sem,
            recv_sem=recv_sem.at[k >> 5], device_id=(th, tc), device_id_type=MESH,
        ).start()
        return 0

    lax.fori_loop(1, FIRST, send, 0, unroll=5)
    pltpu.make_async_copy(id_near.at[pl.ds(0, 3)], id_near.at[pl.ds(0, 3)], idsend_sem.at[0]).wait()
    pltpu.make_async_copy(id_near.at[pl.ds(0, 3)], id_near.at[pl.ds(0, 3)], idrecv_sem.at[0]).wait()
    for v in range(4):
        for h in range(4):
            row = id_near[h]
            id_send[v, h] = pltpu.roll(row, 32 * v, axis=1) if v else row
    id_recv[ci] = id_near[...]

    def send_ids(k, _):
        c = (ci + k) & 31
        pltpu.make_async_remote_copy(
            src_ref=id_send.at[k & 3], dst_ref=id_recv.at[ci], send_sem=idsend_sem.at[1], recv_sem=idrecv_sem.at[1],
            device_id=(hi, c), device_id_type=MESH,
        ).start()
        return 0

    lax.fori_loop(1, 32, send_ids, 0)
    lax.fori_loop(FIRST, SECOND, send, 0, unroll=8)

    ia, ib = iota((LANES, LANES), 0), iota((LANES, LANES), 1)
    same_part = (ia >= 64) & (ib >= 64) & (ia < 96) & (ib < 96) & ((ia < 80) == (ib < 80))
    penalty = jnp.where(same_part & (jnp.abs(ia - ib) > 1), BIG, 0.0).astype(jnp.bfloat16)

    lax.fori_loop(SECOND, THIRD, send, 0, unroll=8)
    m_buf[...] = jnp.full(m_buf.shape, BIG, jnp.float32)
    acc_buf[...] = jnp.zeros(acc_buf.shape, jnp.float32)

    pltpu.make_async_copy(id_recv.at[pl.ds(0, 31)], id_recv.at[pl.ds(0, 31)], idsend_sem.at[1]).wait()
    pltpu.make_async_copy(id_recv.at[pl.ds(0, 31)], id_recv.at[pl.ds(0, 31)], idrecv_sem.at[1]).wait()

    def code(g):
        tile_no = iota((256, LANES), 0).astype(jnp.float32)
        hots = []
        for part in range(GROUP // 4):
            cell_ids = 0.0
            for r in range(4):
                sh, sc = source(g * GROUP + 4 * part + r)
                cell_ids = cell_ids + id_recv[sc, sh]
            hots.append(jnp.where(tile_no == cell_ids, 1.0, 0.0).astype(jnp.bfloat16))
        codes = dot(table_buf[...], jnp.concatenate(hots, axis=1)).T.astype(jnp.bfloat16)
        k_buf[pl.ds(g * GROUP, GROUP)] = codes.reshape(GROUP, ROWS, LANES)
        q_buf[pl.ds(g * GROUP, GROUP)] = dot(codes, penalty).astype(jnp.bfloat16).reshape(GROUP, ROWS, LANES)
        v_buf[g, 64:80, :] = jnp.ones((16, CELLS), jnp.bfloat16)

    code(0)

    def prepare(g):
        @pl.when(g < STEPS)
        def _():
            for i in range(PER_STEP):
                send(THIRD + g * PER_STEP + i, 0)

        pltpu.make_async_copy(recv_buf.at[pl.ds(0, GROUP)], recv_buf.at[pl.ds(0, GROUP)], recv_sem.at[g]).wait()
        slots = pl.ds(g * GROUP, GROUP)
        low = iota((GROUP, ROWS, LANES), 2) < HD
        low_half = iota((GROUP, HALF, LANES), 2) < HD
        kv = recv_buf[slots, 16:48]
        qq = recv_buf[slots, 0:16]
        qr = pltpu.roll(qq.astype(jnp.float32).reshape(GROUP * HALF, LANES), HD, axis=1)
        qr = qr.astype(jnp.bfloat16).reshape(GROUP, HALF, LANES)
        v_buf[g, 0:64, :] = kv.reshape(CELLS, LANES).astype(jnp.float32).T[64:128].astype(jnp.bfloat16)
        k_buf[slots] = jnp.where(low, kv, k_buf[slots])
        q_buf[slots, 0:16] = jnp.where(low_half, qq, q_buf[slots, 0:16])
        q_buf[slots, 16:32] = jnp.where(low_half, qr, q_buf[slots, 16:32])

    def score(item, slot):
        t, j = item
        q = q_buf[pl.ds(t * QT, QT)].reshape(QC, LANES)
        k = k_buf[pl.ds(j * GROUP, GROUP)].reshape(CELLS, LANES)
        s_buf[slot] = dot_t(k, q)

    def update(item, slot, following=None):
        t, j = item
        if following is not None:
            score(following, 1 - slot)
        s = s_buf[slot]
        m_old = m_buf[t]
        m_new = jnp.maximum(m_old, jnp.max(s, axis=0, keepdims=True))
        w = jnp.exp2(s - m_new[0:1]).astype(jnp.bfloat16)
        acc = acc_buf[t] * jnp.exp2(m_old - m_new)[0:1] + dot(v_buf[j], w)
        m_buf[t] = m_new
        acc_buf[t] = acc

    def pack(t):
        acc = acc_buf[t]
        res = acc[0:64] / acc[64:65]
        res = jnp.concatenate([res, res], axis=0).T.reshape(QT, ROWS, LANES)
        lo = iota((QT, HALF, LANES), 2) < HD
        osend_buf[pl.ds(t * QT, QT)] = jnp.where(lo, res[:, 0:16], res[:, 16:32]).astype(jnp.bfloat16)

    def give(t):
        def one(k):
            pltpu.make_async_remote_copy(
                src_ref=osend_buf.at[k], dst_ref=orecv_buf.at[me >> 4, me & 15], send_sem=osend_sem,
                recv_sem=orecv_sem, device_id=source(k), device_id_type=MESH,
            ).start()

        @pl.when(t > 0)
        def _():
            one(t * QT)

        @pl.when(t == 0)
        def _():
            pltpu.make_async_copy(osend_buf.at[0], orecv_buf.at[me >> 4, me & 15], orecv_sem).start()

        for i in range(1, QT):
            one(t * QT + i)

    def group_step(g, _):
        prepare(g)

        def item(i):
            r = i - 2 * g
            return (jnp.where(r < 0, i, 2 * g + (r & 1)), jnp.where(r < 0, g, r >> 1))

        score(item(0), 0)

        def two(i, _):
            update(item(2 * i), 0, item(2 * i + 1))
            update(item(2 * i + 1), 1, item(2 * i + 2))
            return 0

        lax.fori_loop(0, 2 * g, two, 0)
        update(item(4 * g), 0, item(4 * g + 1))
        update(item(4 * g + 1), 1)
        code(g + 1)
        return 0

    last = NGROUP - 1
    lax.fori_loop(0, last, group_step, 0)
    prepare(last)
    score((0, last), 0)
    update((0, last), 0, (1, last))

    def two_old(i, _):
        update((2 * i + 1, last), 1, (2 * i + 2, last))
        pack(2 * i)
        give(2 * i)
        update((2 * i + 2, last), 0, (2 * i + 3, last))
        pack(2 * i + 1)
        give(2 * i + 1)
        return 0

    lax.fori_loop(0, last - 1, two_old, 0)
    items = [(2 * last - 1, last)] + [(t, j) for t in (2 * last, 2 * last + 1) for j in range(NGROUP)]
    done = 2 * last - 2
    for i, it in enumerate(items):
        update(it, (i + 1) & 1, items[i + 1] if i + 1 < len(items) else None)
        if it[1] == 0 or i == 0:
            pack(done)
            give(done)
            done += 1
    pack(done)
    give(done)

    pltpu.make_async_copy(orecv_buf, orecv_buf, orecv_sem).wait()
    lo = iota((GENES, HALF, LANES), 2) < HD
    for p in range(HEADS // 2):
        even = orecv_buf[:, 2 * p].astype(jnp.float32)
        odd = orecv_buf[:, 2 * p + 1].astype(jnp.float32)
        swap = lambda a: pltpu.roll(a.reshape(GENES * HALF, LANES), HD, axis=1).reshape(GENES, HALF, LANES)
        att_buf[:, 0:16, 128 * p : 128 * p + 128] = jnp.where(lo, even, swap(odd)).astype(jnp.bfloat16)
        att_buf[:, 16:32, 128 * p : 128 * p + 128] = jnp.where(lo, swap(even), odd).astype(jnp.bfloat16)
    pltpu.make_async_copy(recv_buf.at[pl.ds(0, NDEV - 1)], recv_buf.at[pl.ds(0, NDEV - 1)], send_sem).wait()
    pltpu.make_async_copy(osend_buf.at[pl.ds(0, 127)], osend_buf.at[pl.ds(0, 127)], osend_sem).wait()


def on_device(cells_in, gain, w_qkv, w_out, tile_of_cell, tile_adjacent):
    bf, f32 = jnp.bfloat16, jnp.float32
    vm = pltpu.VMEM
    hbm = pl.BlockSpec(memory_space=pl.ANY)
    vmem = pl.BlockSpec(memory_space=pltpu.VMEM)
    attended = pl.pallas_call(
        kernel,
        out_shape=jax.ShapeDtypeStruct(cells_in.shape, bf),
        in_specs=[hbm, vmem, hbm, vmem, vmem],
        out_specs=vmem,
        scratch_shapes=[
            vm((GENES, ROWS, 1024), bf),
            vm((12, 1024, 256), bf),
            vm((GENES * ROWS, 1024), bf),
            vm((GENES, HEADS, 48, LANES), bf),
            vm((NDEV, 48, LANES), bf),
            vm((4, 1, LANES), f32),
            vm((4, 4, 1, LANES), f32),
            vm((32, 4, 1, LANES), f32),
            vm((LANES, 256), bf),
            vm((NDEV, ROWS, LANES), bf),
            vm((NDEV, ROWS, LANES), bf),
            vm((NGROUP, 80, CELLS), bf),
            vm((2, CELLS, QC), f32),
            vm((NT, 8, QC), f32),
            vm((NT, 80, QC), f32),
            vm((NDEV, HALF, LANES), bf),
            vm((GENES, HEADS, HALF, LANES), bf),
            pltpu.SemaphoreType.DMA,
            pltpu.SemaphoreType.DMA((12,)),
            pltpu.SemaphoreType.DMA,
            pltpu.SemaphoreType.DMA((NGROUP,)),
            pltpu.SemaphoreType.DMA((2,)),
            pltpu.SemaphoreType.DMA((2,)),
            pltpu.SemaphoreType.DMA,
            pltpu.SemaphoreType.DMA,
        ],
        compiler_params=pltpu.CompilerParams(
            collective_id=0, has_side_effects=True, vmem_limit_bytes=56 * 1024 * 1024
        ),
    )(cells_in, gain.reshape(1, -1), w_qkv, tile_of_cell.reshape(1, -1), tile_adjacent)
    return jnp.dot(attended, w_out, preferred_element_type=jnp.float32).astype(bf)


def solution(mesh):
    return jax.shard_map(
        on_device,
        mesh=mesh,
        in_specs=(P(None, ("heads", "cells"), None), P(), P(), P(), P(("heads", "cells")), P()),
        out_specs=P(None, ("heads", "cells"), None),
        check_vma=False,
    )
```

```python
import functools
import math

import jax
import jax.numpy as jnp
from jax import lax
from jax.experimental import pallas as pl
from jax.experimental.pallas import tpu as pltpu
from jax.sharding import PartitionSpec as P

MESH = pl.DeviceIdType.MESH
HD = 64
NDEV = 128
GENES = 8
HEADS = 16
ROWS = 32
HALF = 16
LANES = 128
GROUP = 32
NGROUP = NDEV // GROUP
FIRST, SECOND, THIRD = 16, 32, 64
STEPS = 2
PER_STEP = (NDEV - THIRD) // STEPS
CELLS = GROUP * ROWS
QT = 16
QC = QT * ROWS
NT = NDEV // QT
BIG = -1e30
QSCALE = 0.125 * math.log2(math.e)


def iota(shape, dim):
    return lax.broadcasted_iota(jnp.int32, shape, dim)


def dot(a, b):
    return jnp.dot(a, b, preferred_element_type=jnp.float32)


def dot_t(a, b):
    return lax.dot_general(a, b, (((1,), (1,)), ((), ())), preferred_element_type=jnp.float32)


def grid_places(adj):
    n = adj.shape[0]
    fi = lambda shape, dim: iota(shape, dim).astype(jnp.float32)
    degree = dot(jnp.ones((8, n), jnp.bfloat16), adj)
    corner = degree == 4.0
    before = (iota((n, n), 0) < iota((n, n), 1)).astype(jnp.bfloat16)
    order = dot(corner.astype(jnp.float32).astype(jnp.bfloat16), before)
    reach = jnp.where(corner & (order == fi((8, n), 0)), 1.0, 0.0)

    def step(_, state):
        reach, dist = state
        dist = dist + (1.0 - reach)
        return jnp.minimum(dot(reach.astype(jnp.bfloat16), adj), 1.0), dist

    dist = jnp.zeros((8, n), jnp.float32)
    for i in range(14):
        reach, dist = step(i, (reach, dist))
    dist = dist + (1.0 - reach)
    d0, d1, d2, d3 = (dist[i : i + 1] for i in range(4))
    on_path = lambda d: jnp.sum(jnp.where(d0 + d == 15.0, 1.0, 0.0), axis=1, keepdims=True)
    opp1, opp2 = on_path(d1) == 16.0, on_path(d2) == 16.0
    far = jnp.where(opp1, d1, jnp.where(opp2, d2, d3))
    side = jnp.where(opp1, d2, d1)
    other = jnp.where(opp1, d3, jnp.where(opp2, d3, d2))
    near = jnp.minimum(d0, side)
    row = jnp.where(near >= 8.0, near, 15.0 - jnp.minimum(other, far))
    near = jnp.minimum(d0, other)
    col = jnp.where(near >= 8.0, near, 15.0 - jnp.minimum(side, far))
    return row, col


def kernel(
    x_hbm, gain_ref, wqkv_hbm, ids_ref, adj_ref, att_buf,
    x_buf, w_buf, norm_buf, send_buf, recv_buf, id_near, id_send, id_recv, table_buf,
    q_buf, k_buf, v_buf, s_buf, m_buf, acc_buf, osend_buf, orecv_buf,
    x_sem, w_sem, send_sem, recv_sem, idsend_sem, idrecv_sem, osend_sem, orecv_sem,
):
    hi = lax.axis_index("heads")
    ci = lax.axis_index("cells")
    me = hi * 32 + ci

    def device(p):
        return (p >> 5, p & 31)

    z, y, x, core = ci >> 3, ci & 3, (hi & 2) | ((ci >> 2) & 1), hi & 1

    def moved(k, i, sign):
        dx, dy = i >> 2, i & 3
        b = k >> 4
        px, py, pz = (x + sign * dx) & 3, (y + sign * dy) & 3, (z + sign * ((b >> 1) + dx + dy)) & 3
        return ((px & 2) | (core ^ (b & 1)), pz * 8 + (px & 1) * 4 + py)

    def target(k, i):
        return moved(k, i, 1)

    def source(k, i):
        return moved(k, i, -1)

    x_copy = pltpu.make_async_copy(x_hbm, x_buf, x_sem)
    x_copy.start()
    w_copies = []
    for c in range(4):
        for part in range(3):
            cp = pltpu.make_async_copy(
                wqkv_hbm.at[:, pl.ds(part * 1024 + c * 256, 256)], w_buf.at[c * 3 + part], w_sem.at[c * 3 + part]
            )
            cp.start()
            w_copies.append(cp)

    barrier = pltpu.get_barrier_semaphore()

    def greet(k, _):
        pl.semaphore_signal(barrier, inc=1, device_id=device((me + k) & 127), device_id_type=MESH)
        return 0

    lax.fori_loop(1, NDEV, greet, 0)

    ids = ids_ref[...].astype(jnp.float32)
    id_near[hi] = jnp.concatenate([ids, jnp.zeros((1, 96), jnp.float32)], axis=1)

    x_copy.wait()
    x32 = x_buf[...].reshape(GENES * ROWS, 1024).astype(jnp.float32)
    mean = jnp.mean(x32 * x32, axis=-1, keepdims=True)
    norm_buf[...] = (x32 * lax.rsqrt(mean + 1e-05) * gain_ref[...]).astype(jnp.bfloat16)

    low = iota((GENES, ROWS, LANES), 2) < HD
    low_half = iota((GENES, HALF, LANES), 2) < HD
    xn = norm_buf[...]
    for cp in w_copies:
        cp.wait()
    row, col = grid_places(adj_ref[...].astype(jnp.float32).astype(jnp.bfloat16))
    place = iota((LANES, 256), 0).astype(jnp.float32)
    table_buf[...] = jnp.where((place == row + 64.0) | (place == col + 80.0), 1.0, 0.0).astype(jnp.bfloat16)
    for c in range(4):
        q4 = dot(xn, w_buf[c * 3]) * QSCALE
        k4 = dot(xn, w_buf[c * 3 + 1])
        v4 = dot(xn, w_buf[c * 3 + 2])
        for p in range(2):
            cut = lambda a: a[:, 128 * p : 128 * p + 128]
            swap = lambda a: pltpu.roll(a, HD, axis=1).reshape(GENES, ROWS, LANES)
            as3 = lambda a: a.reshape(GENES, ROWS, LANES)
            q2, k2, v2 = cut(q4), cut(k4), cut(v4)
            qs, ks, vs = swap(q2), swap(k2), swap(v2)
            q2, k2, v2 = as3(q2), as3(k2), as3(v2)
            head = 4 * c + 2 * p
            send_buf[:, head, 0:16, :] = jnp.where(low_half, q2[:, 0:16], qs[:, 16:32]).astype(jnp.bfloat16)
            send_buf[:, head, 16:48, :] = jnp.where(low, k2, vs).astype(jnp.bfloat16)
            send_buf[:, head + 1, 0:16, :] = jnp.where(low_half, qs[:, 0:16], q2[:, 16:32]).astype(jnp.bfloat16)
            send_buf[:, head + 1, 16:48, :] = jnp.where(low, ks, v2).astype(jnp.bfloat16)

    own = pltpu.make_async_copy(send_buf.at[me >> 4, me & 15], recv_buf.at[0], recv_sem.at[0])
    own.start()
    pl.semaphore_wait(barrier, NDEV - 1)

    def id_copy_near(k):
        return pltpu.make_async_remote_copy(
            src_ref=id_near.at[hi], dst_ref=id_near.at[hi], send_sem=idsend_sem.at[0], recv_sem=idrecv_sem.at[0],
            device_id=((hi + k) & 3, ci), device_id_type=MESH,
        )

    for k in range(1, 4):
        id_copy_near(k).start()

    def send(k):
        th, tc = target(k, k & 15)
        pltpu.make_async_remote_copy(
            src_ref=send_buf.at[th * 2 + (tc >> 4), tc & 15], dst_ref=recv_buf.at[k], send_sem=send_sem,
            recv_sem=recv_sem.at[k >> 5], device_id=(th, tc), device_id_type=MESH,
        ).start()

    def send_range(start, stop):
        for k in range(start, stop):
            send(k)

    send_range(1, FIRST)
    pltpu.make_async_copy(id_near.at[pl.ds(0, 3)], id_near.at[pl.ds(0, 3)], idsend_sem.at[0]).wait()
    pltpu.make_async_copy(id_near.at[pl.ds(0, 3)], id_near.at[pl.ds(0, 3)], idrecv_sem.at[0]).wait()
    for v in range(4):
        for h in range(4):
            row = id_near[h]
            id_send[v, h] = pltpu.roll(row, 32 * v, axis=1) if v else row
    id_recv[ci] = id_near[...]

    def send_ids(k, _):
        c = (ci + k) & 31
        pltpu.make_async_remote_copy(
            src_ref=id_send.at[k & 3], dst_ref=id_recv.at[ci], send_sem=idsend_sem.at[1], recv_sem=idrecv_sem.at[1],
            device_id=(hi, c), device_id_type=MESH,
        ).start()
        return 0

    lax.fori_loop(1, 32, send_ids, 0)
    send_range(FIRST, SECOND)

    ia, ib = iota((LANES, LANES), 0), iota((LANES, LANES), 1)
    same_part = (ia >= 64) & (ib >= 64) & (ia < 96) & (ib < 96) & ((ia < 80) == (ib < 80))
    penalty = jnp.where(same_part & (jnp.abs(ia - ib) > 1), BIG, 0.0).astype(jnp.bfloat16)

    send_range(SECOND, THIRD)
    m_buf[...] = jnp.full(m_buf.shape, BIG, jnp.float32)
    acc_buf[...] = jnp.zeros(acc_buf.shape, jnp.float32)

    pltpu.make_async_copy(id_recv.at[pl.ds(0, 31)], id_recv.at[pl.ds(0, 31)], idsend_sem.at[1]).wait()
    pltpu.make_async_copy(id_recv.at[pl.ds(0, 31)], id_recv.at[pl.ds(0, 31)], idrecv_sem.at[1]).wait()

    def code(g):
        tile_no = iota((256, LANES), 0).astype(jnp.float32)
        hots = []
        for part in range(GROUP // 4):
            cell_ids = 0.0
            for r in range(4):
                sh, sc = source(g * GROUP + 4 * part + r, (4 * part + r) & 15)
                cell_ids = cell_ids + id_recv[sc, sh]
            hots.append(jnp.where(tile_no == cell_ids, 1.0, 0.0).astype(jnp.bfloat16))
        codes = dot(table_buf[...], jnp.concatenate(hots, axis=1)).T.astype(jnp.bfloat16)
        k_buf[pl.ds(g * GROUP, GROUP)] = codes.reshape(GROUP, ROWS, LANES)
        q_buf[pl.ds(g * GROUP, GROUP)] = dot(codes, penalty).astype(jnp.bfloat16).reshape(GROUP, ROWS, LANES)
        v_buf[g, 64:80, :] = jnp.ones((16, CELLS), jnp.bfloat16)

    code(0)

    def prepare(g):
        for step in range(STEPS):

            @pl.when(g == step)
            def _():
                send_range(THIRD + step * PER_STEP, THIRD + (step + 1) * PER_STEP)

        pltpu.make_async_copy(recv_buf.at[pl.ds(0, GROUP)], recv_buf.at[pl.ds(0, GROUP)], recv_sem.at[g]).wait()
        slots = pl.ds(g * GROUP, GROUP)
        low = iota((GROUP, ROWS, LANES), 2) < HD
        low_half = iota((GROUP, HALF, LANES), 2) < HD
        kv = recv_buf[slots, 16:48]
        qq = recv_buf[slots, 0:16]
        qr = pltpu.roll(qq.astype(jnp.float32).reshape(GROUP * HALF, LANES), HD, axis=1)
        qr = qr.astype(jnp.bfloat16).reshape(GROUP, HALF, LANES)
        v_buf[g, 0:64, :] = kv.reshape(CELLS, LANES).astype(jnp.float32).T[64:128].astype(jnp.bfloat16)
        k_buf[slots] = jnp.where(low, kv, k_buf[slots])
        q_buf[slots, 0:16] = jnp.where(low_half, qq, q_buf[slots, 0:16])
        q_buf[slots, 16:32] = jnp.where(low_half, qr, q_buf[slots, 16:32])

    def score(item, slot):
        t, j = item
        q = q_buf[pl.ds(t * QT, QT)].reshape(QC, LANES)
        k = k_buf[pl.ds(j * GROUP, GROUP)].reshape(CELLS, LANES)
        s_buf[slot] = dot_t(k, q)

    def update(item, slot, following=None):
        t, j = item
        if following is not None:
            score(following, 1 - slot)
        s = s_buf[slot]
        m_old = m_buf[t]
        m_new = jnp.maximum(m_old, jnp.max(s, axis=0, keepdims=True))
        w = jnp.exp2(s - m_new[0:1]).astype(jnp.bfloat16)
        acc = acc_buf[t] * jnp.exp2(m_old - m_new)[0:1] + dot(v_buf[j], w)
        m_buf[t] = m_new
        acc_buf[t] = acc

    def pack(t):
        acc = acc_buf[t]
        res = acc[0:64] / acc[64:65]
        res = jnp.concatenate([res, res], axis=0).T.reshape(QT, ROWS, LANES)
        lo = iota((QT, HALF, LANES), 2) < HD
        osend_buf[pl.ds(t * QT, QT)] = jnp.where(lo, res[:, 0:16], res[:, 16:32]).astype(jnp.bfloat16)

    def give(t):
        def one(i):
            k = t * QT + i
            pltpu.make_async_remote_copy(
                src_ref=osend_buf.at[k], dst_ref=orecv_buf.at[me >> 4, me & 15], send_sem=osend_sem,
                recv_sem=orecv_sem, device_id=source(k, i), device_id_type=MESH,
            ).start()

        @pl.when(t > 0)
        def _():
            one(0)

        @pl.when(t == 0)
        def _():
            pltpu.make_async_copy(osend_buf.at[0], orecv_buf.at[me >> 4, me & 15], orecv_sem).start()

        for i in range(1, QT):
            one(i)

    def group_step(g, _):
        prepare(g)

        def item(i):
            r = i - 2 * g
            return (jnp.where(r < 0, i, 2 * g + (r & 1)), jnp.where(r < 0, g, r >> 1))

        score(item(0), 0)

        def two(i, _):
            update(item(2 * i), 0, item(2 * i + 1))
            update(item(2 * i + 1), 1, item(2 * i + 2))
            return 0

        lax.fori_loop(0, 2 * g, two, 0)
        update(item(4 * g), 0, item(4 * g + 1))
        update(item(4 * g + 1), 1)
        code(g + 1)
        return 0

    last = NGROUP - 1
    lax.fori_loop(0, last, group_step, 0)
    prepare(last)
    score((0, last), 0)
    update((0, last), 0, (1, last))

    def two_old(i, _):
        update((2 * i + 1, last), 1, (2 * i + 2, last))
        pack(2 * i)
        give(2 * i)
        update((2 * i + 2, last), 0, (2 * i + 3, last))
        pack(2 * i + 1)
        give(2 * i + 1)
        return 0

    lax.fori_loop(0, last - 1, two_old, 0)
    items = [(2 * last - 1, last)] + [(t, j) for t in (2 * last, 2 * last + 1) for j in range(NGROUP)]
    done = 2 * last - 2
    for i, it in enumerate(items):
        update(it, (i + 1) & 1, items[i + 1] if i + 1 < len(items) else None)
        if it[1] == 0 or i == 0:
            pack(done)
            give(done)
            done += 1
    pack(done)
    give(done)

    pltpu.make_async_copy(orecv_buf, orecv_buf, orecv_sem).wait()
    lo = iota((GENES, HALF, LANES), 2) < HD
    for p in range(HEADS // 2):
        even = orecv_buf[:, 2 * p].astype(jnp.float32)
        odd = orecv_buf[:, 2 * p + 1].astype(jnp.float32)
        swap = lambda a: pltpu.roll(a.reshape(GENES * HALF, LANES), HD, axis=1).reshape(GENES, HALF, LANES)
        att_buf[:, 0:16, 128 * p : 128 * p + 128] = jnp.where(lo, even, swap(odd)).astype(jnp.bfloat16)
        att_buf[:, 16:32, 128 * p : 128 * p + 128] = jnp.where(lo, swap(even), odd).astype(jnp.bfloat16)
    pltpu.make_async_copy(recv_buf.at[pl.ds(0, NDEV - 1)], recv_buf.at[pl.ds(0, NDEV - 1)], send_sem).wait()
    pltpu.make_async_copy(osend_buf.at[pl.ds(0, 127)], osend_buf.at[pl.ds(0, 127)], osend_sem).wait()


def on_device(cells_in, gain, w_qkv, w_out, tile_of_cell, tile_adjacent):
    bf, f32 = jnp.bfloat16, jnp.float32
    vm = pltpu.VMEM
    hbm = pl.BlockSpec(memory_space=pl.ANY)
    vmem = pl.BlockSpec(memory_space=pltpu.VMEM)
    attended = pl.pallas_call(
        kernel,
        out_shape=jax.ShapeDtypeStruct(cells_in.shape, bf),
        in_specs=[hbm, vmem, hbm, vmem, vmem],
        out_specs=vmem,
        scratch_shapes=[
            vm((GENES, ROWS, 1024), bf),
            vm((12, 1024, 256), bf),
            vm((GENES * ROWS, 1024), bf),
            vm((GENES, HEADS, 48, LANES), bf),
            vm((NDEV, 48, LANES), bf),
            vm((4, 1, LANES), f32),
            vm((4, 4, 1, LANES), f32),
            vm((32, 4, 1, LANES), f32),
            vm((LANES, 256), bf),
            vm((NDEV, ROWS, LANES), bf),
            vm((NDEV, ROWS, LANES), bf),
            vm((NGROUP, 80, CELLS), bf),
            vm((2, CELLS, QC), f32),
            vm((NT, 8, QC), f32),
            vm((NT, 80, QC), f32),
            vm((NDEV, HALF, LANES), bf),
            vm((GENES, HEADS, HALF, LANES), bf),
            pltpu.SemaphoreType.DMA,
            pltpu.SemaphoreType.DMA((12,)),
            pltpu.SemaphoreType.DMA,
            pltpu.SemaphoreType.DMA((NGROUP,)),
            pltpu.SemaphoreType.DMA((2,)),
            pltpu.SemaphoreType.DMA((2,)),
            pltpu.SemaphoreType.DMA,
            pltpu.SemaphoreType.DMA,
        ],
        compiler_params=pltpu.CompilerParams(
            collective_id=0, has_side_effects=True, vmem_limit_bytes=56 * 1024 * 1024
        ),
    )(cells_in, gain.reshape(1, -1), w_qkv, tile_of_cell.reshape(1, -1), tile_adjacent)
    return jnp.dot(attended, w_out, preferred_element_type=jnp.float32).astype(bf)


def solution(mesh):
    return jax.shard_map(
        on_device,
        mesh=mesh,
        in_specs=(P(None, ("heads", "cells"), None), P(), P(), P(), P(("heads", "cells")), P()),
        out_specs=P(None, ("heads", "cells"), None),
        check_vma=False,
    )
```
